32 devices in a mesh: exp: 16 (over z, x, core), ctx: 2 (over y).
Axes of the slice: x: 2, y: 2, z: 4, core: 2. Of those that a mesh axis runs over, the one named last changes fastest.
Arguments:
- y_first: bfloat16 [2048, 1024], P('exp', 'ctx'), may hold values from -6 to 6
- y_second: bfloat16 [2048, 1024], P('exp', 'ctx'), may hold values from -6 to 6
- grad_first: bfloat16 [2048, 1024], P('exp', 'ctx'), may hold values from -6 to 6
- grad_second: bfloat16 [2048, 1024], P('exp', 'ctx'), may hold values from -6 to 6
- expert_ids: int32 [2048, 6], P('exp'), may hold values from 0 to 15, all different within a row; in each aligned block of 128 rows (0 to 127, 128 to 255, ...) at most 64 rows name the same one
- gate_fixed: int32 [2048, 6], P('exp'), may hold values from 4096 to 65535
- gain_attn: float32 [1024], replicated, may hold values from 0.5 to 1.5
- gain_latent: float32 [512], replicated, may hold values from 0.5 to 1.5
- gain_moe: float32 [1024], replicated, may hold values from 0.5 to 1.5
- w_query: bfloat16 [1024, 1024], P(None, 'ctx'), may hold values from -0.1875 to 0.1875
- w_latent: bfloat16 [1024, 512], P(None, 'ctx'), may hold values from -0.1875 to 0.1875
- w_key_up: bfloat16 [512, 1024], P(None, 'ctx'), may hold values from -0.25 to 0.25
- w_value_up: bfloat16 [512, 1024], P(None, 'ctx'), may hold values from -0.25 to 0.25
- w_out: bfloat16 [1024, 1024], P('ctx'), may hold values from -0.1875 to 0.1875
- w_gate: bfloat16 [16, 1024, 1408], P('exp', None, 'ctx'), may hold values from -0.1875 to 0.1875
- w_up: bfloat16 [16, 1024, 1408], P('exp', None, 'ctx'), may hold values from -0.1875 to 0.1875
- w_down: bfloat16 [16, 1408, 1024], P('exp', 'ctx'), may hold values from -0.15625 to 0.15625
Outputs:
- first_out: bfloat16 [2048, 1024], P('exp', 'ctx')
- second_out: bfloat16 [2048, 1024], P('exp', 'ctx')
- grad_first_out: bfloat16 [2048, 1024], P('exp', 'ctx')
- grad_second_out: bfloat16 [2048, 1024], P('exp', 'ctx')
The draws below stay inside these ranges and needn't reach their ends.
Inputs may be any that keep to these rules, and one draw needn't show every extreme that they name: `expert_ids`: each row names 6 different experts. In each aligned block of 128 rows (one window, the rows of one index of exp) no expert is named by more than 64 rows, a bound that some expert reaches in every block.
All inputs are finite; a program needn't handle non-finite values.
Results may differ from the reference program's by a relative error of at most 0.025.
Values may be sent and summed in bfloat16 or wider, within the bound.
No kernel may reach another device: no remote copies, remote signals or barrier semaphores. Data moves between devices by JAX's collectives and lax.ppermute only.
A program may use at most 64 MiB of HBM per device.

```python
import math
import jax
import jax.numpy as jnp
import numpy as np
from jax import lax

D = 1024
FF = 1408
LAT = 512
HEAD_DIM = 128
HEADS = 8
TOP = 6
EXPERTS = 16
WINDOW = 128
TOKENS = 2048
CAP = 64
N_CTX = 2


def plant(drawn, own_key, low, high):
    longest = drawn.shape.index(max(drawn.shape))
    spots = []
    for shift in (0, 1):
        where = [jax.random.randint(jax.random.fold_in(own_key, axis), (), 0, length) for axis, length in enumerate(drawn.shape)]
        where[longest] = (where[longest] + shift) % drawn.shape[longest]
        spots.append(tuple(where))
    return drawn.at[spots[0]].set(low).at[spots[1]].set(high)


def block_levels(key, extent, split, least, top_value):
    gain = 1.0
    for position, parts in split:
        steps = jax.random.uniform(jax.random.fold_in(jax.random.fold_in(key, 6), position), (parts,), jnp.float32, least / len(split), top_value / len(split))
        gain = gain * jnp.repeat(jnp.exp(steps), extent[position] // parts).reshape((-1,) + (1,) * (len(extent) - 1 - position))
    return gain


def deal_out(key, own, number, rows, count, top, limit, lean):
    order = jax.random.permutation(key, count)
    packed, usual = load_shares(count, rows * top, limit, lean, True), load_shares(count, rows * top, limit, lean, False)
    places = jnp.arange(count)

    def named(tallies, turn):
        used = int((tallies > 0).sum())
        fixed = max(1, used // 4)
        passed = fixed + (places - fixed + turn * (used - fixed)) % max(1, count - fixed)
        return jnp.zeros((count,), jnp.int32).at[order[jnp.where(places < fixed, places, passed)]].set(jnp.asarray(tallies, jnp.int32))

    tallies = jnp.where(number % 4 == 0, named(packed, number // 4), named(usual, number - number // 4 - 1))
    mixed = jax.random.permutation(jax.random.fold_in(own, 3), count)
    donor, taker = mixed[0:count // 2 * 2:2], mixed[1:count // 2 * 2:2]
    room = jnp.minimum(tallies[donor] - 1, limit - tallies[taker]) // 2
    room = jnp.where((donor == order[0]) | (taker == order[0]) | (tallies[taker] == 0), 0, jnp.maximum(room, 0))
    passed = jax.random.randint(jax.random.fold_in(own, 4), (count // 2,), 0, 1 << 20) % (room + 1)
    tallies = tallies.at[donor].add(-passed).at[taker].add(passed)
    members = jnp.searchsorted(jnp.cumsum(tallies), jnp.arange(rows * top), side="right").astype(jnp.int32)
    listing = members.reshape(top, rows).T
    listing = listing[jax.random.permutation(jax.random.fold_in(own, 1), rows)]
    turn = jax.random.randint(jax.random.fold_in(own, 2), (rows, 1), 0, top)
    return jnp.take_along_axis(listing, (jnp.arange(top)[None, :] + turn) % top, axis=1)


def load_shares(count, total, limit, slope, full):
    loads = [(1 << 20) // math.isqrt(grade ** slope) + 1 for grade in range(1, count + 1)]
    largest = limit if full else min(limit, max(-(-total // count), total * loads[0] // sum(loads)))
    least = 1 if total - largest >= count - 1 else 0
    counts, rest = [largest] + [least] * (count - 1), total - largest - least * (count - 1)
    while rest > 0:
        free = [i for i in range(1, count) if counts[i] < largest] or [i for i in range(1, count) if counts[i] < limit]
        mass, left = sum([loads[i] for i in free]), rest
        for i in free:
            addition = min(limit - counts[i], max(1, left * loads[i] // mass), rest)
            counts[i] = counts[i] + addition
            rest = rest - addition
    return np.array(counts)


def gaussian(stream_key, dims, spread, bound, split=(), dtype=jnp.bfloat16):
    result = jax.random.normal(stream_key, dims, jnp.float32) * spread
    if len(split) > 0:
        result = block_levels(stream_key, dims, split, -0.22, 0.18) * result
    return jnp.clip(result, min=-bound, max=bound).astype(dtype)


def setup_inputs(seed: int = 0) -> dict:
    keys = jax.random.split(jax.random.key(seed), 18)
    y_first = gaussian(keys[0], (TOKENS, D), 1.0, 6.0, ((0, 16), (1, 2)))
    y_second = gaussian(keys[1], (TOKENS, D), 1.0, 6.0, ((0, 16), (1, 2)))
    grad_first = gaussian(keys[2], (TOKENS, D), 1.0, 6.0, ((0, 16), (1, 2)))
    grad_second = gaussian(keys[3], (TOKENS, D), 1.0, 6.0, ((0, 16), (1, 2)))
    expert_ids_keys = jax.random.split(jax.random.fold_in(keys[4], 1), TOKENS // WINDOW)
    expert_ids_turns = jax.random.permutation(jax.random.fold_in(keys[4], 3), TOKENS // WINDOW)
    expert_ids = jax.vmap(lambda own, number: deal_out(jax.random.fold_in(keys[4], 2), own, number, WINDOW, EXPERTS, TOP, CAP, 2))(expert_ids_keys, expert_ids_turns).reshape((TOKENS, TOP))
    gate_fixed = plant(jax.random.randint(keys[5], (TOKENS, TOP), 4096, 65536), jax.random.fold_in(keys[5], 1), 4096, 65535).astype(jnp.int32)
    gain_attn = jnp.clip(1.0 + 0.1 * jax.random.normal(keys[6], (D,), jnp.float32), 0.5, 1.5)
    gain_latent = jnp.clip(1.0 + 0.1 * jax.random.normal(keys[7], (LAT,), jnp.float32), 0.5, 1.5)
    gain_moe = jnp.clip(1.0 + 0.1 * jax.random.normal(keys[8], (D,), jnp.float32), 0.5, 1.5)
    w_query = gaussian(keys[9], (D, HEADS * HEAD_DIM), D ** -0.5, 0.1875, ((1, 2),))
    w_latent = gaussian(keys[10], (D, LAT), D ** -0.5, 0.1875, ((1, 2),))
    w_key_up = gaussian(keys[11], (LAT, HEADS * HEAD_DIM), LAT ** -0.5, 0.25, ((1, 2),))
    w_value_up = gaussian(keys[12], (LAT, HEADS * HEAD_DIM), LAT ** -0.5, 0.25, ((1, 2),))
    w_out = gaussian(keys[13], (HEADS * HEAD_DIM, D), (HEADS * HEAD_DIM) ** -0.5, 0.1875, ((0, 2),))
    w_gate = gaussian(keys[14], (EXPERTS, D, FF), D ** -0.5, 0.1875, ((0, 16), (2, 2)))
    w_up = gaussian(keys[15], (EXPERTS, D, FF), D ** -0.5, 0.1875, ((0, 16), (2, 2)))
    w_down = gaussian(keys[16], (EXPERTS, FF, D), FF ** -0.5, 0.15625, ((0, 16), (1, 2)))
    return {"y_first": y_first, "y_second": y_second, "grad_first": grad_first, "grad_second": grad_second, "expert_ids": expert_ids, "gate_fixed": gate_fixed, "gain_attn": gain_attn, "gain_latent": gain_latent, "gain_moe": gain_moe, "w_query": w_query, "w_latent": w_latent, "w_key_up": w_key_up, "w_value_up": w_value_up, "w_out": w_out, "w_gate": w_gate, "w_up": w_up, "w_down": w_down}


epsilon = 1e-06
soft_limit = 5.0

def rounded(values):
    return lax.optimization_barrier(values.astype(jnp.bfloat16)).astype(jnp.float32)

def rms_scale(row_data):
    return lax.rsqrt(lax.optimization_barrier(jnp.mean(row_data * row_data, axis=-1, keepdims=True)) + epsilon)

def rms_back(row_data, gain_vec, grad_in):
    factor = rms_scale(row_data)
    weighted = gain_vec * grad_in
    inner_mean = lax.optimization_barrier(jnp.mean(weighted * row_data, axis=-1, keepdims=True))
    return factor * weighted - row_data * (factor * factor * factor) * inner_mean

def route_slots(expert_rows, expert_count):
    flat_ids = expert_rows.reshape(-1)
    labels = jnp.arange(expert_count).astype(jnp.int32)
    onehot = (flat_ids[:, None] == labels[None, :]).astype(jnp.int32)
    before = (jnp.cumsum(onehot, axis=0) - onehot).astype(jnp.int32)
    return lax.optimization_barrier(jnp.sum(before * onehot, axis=1)).astype(jnp.int32).reshape(expert_rows.shape)

def expert_pass(expert_items):
    slot_rows, slot_grads, gate_mat, up_mat, down_mat = expert_items
    slot_rows = slot_rows.reshape(-1, D).astype(jnp.float32)
    slot_grads = slot_grads.reshape(-1, D).astype(jnp.float32)
    gate_mat = gate_mat.astype(jnp.float32)
    up_mat = up_mat.astype(jnp.float32)
    down_mat = down_mat.astype(jnp.float32)
    slice_width = FF // N_CTX
    gate_proj = jnp.dot(slot_rows, gate_mat, preferred_element_type=jnp.float32)
    up_proj = jnp.dot(slot_rows, up_mat, preferred_element_type=jnp.float32)
    sigmoid_gate = jax.nn.sigmoid(gate_proj)
    hidden = rounded(gate_proj * sigmoid_gate * up_proj)
    pieces = jnp.einsum('rjf,jfd->rjd', hidden.reshape(-1, N_CTX, slice_width), down_mat.reshape(N_CTX, slice_width, D))
    expert_out = lax.optimization_barrier(jnp.sum(rounded(pieces), axis=1))
    grad_hidden = jnp.dot(slot_grads, down_mat.T, preferred_element_type=jnp.float32)
    grad_gate = rounded(grad_hidden * up_proj * sigmoid_gate * (1.0 + gate_proj * (1.0 - sigmoid_gate)))
    grad_up = rounded(grad_hidden * gate_proj * sigmoid_gate)
    back_pieces = jnp.einsum('rjf,djf->rjd', grad_gate.reshape(-1, N_CTX, slice_width), gate_mat.reshape(D, N_CTX, slice_width))
    back_pieces = back_pieces + jnp.einsum('rjf,djf->rjd', grad_up.reshape(-1, N_CTX, slice_width), up_mat.reshape(D, N_CTX, slice_width))
    expert_back = lax.optimization_barrier(jnp.sum(rounded(back_pieces), axis=1))
    return (expert_out, expert_back)

def reference(y_first, y_second, grad_first, grad_second, expert_ids, gate_fixed, gain_attn, gain_latent, gain_moe, w_query, w_latent, w_key_up, w_value_up, w_out, w_gate, w_up, w_down):
    windows = TOKENS // WINDOW
    first_in = y_first.astype(jnp.float32)
    normed = (first_in * rms_scale(first_in) * gain_moe).astype(jnp.bfloat16)
    window_ids = expert_ids.reshape(windows, WINDOW, TOP)
    slot_ids = jax.vmap(lambda part_ids: route_slots(part_ids, EXPERTS))(window_ids)
    window_index = jnp.broadcast_to(jnp.arange(windows).astype(jnp.int32)[:, None, None], window_ids.shape)
    token_index = jnp.broadcast_to(jnp.arange(TOKENS).astype(jnp.int32).reshape(windows, WINDOW)[:, :, None], window_ids.shape)
    empty_buffer = jnp.zeros((EXPERTS, windows, CAP, D), jnp.bfloat16)
    row_buffer = empty_buffer.at[window_ids, window_index, slot_ids].set(normed[token_index])
    grad_buffer = empty_buffer.at[window_ids, window_index, slot_ids].set(grad_second[token_index])
    expert_out, expert_back = lax.map(expert_pass, (row_buffer, grad_buffer, w_gate, w_up, w_down))
    expert_out = expert_out.reshape(EXPERTS, windows, CAP, D)
    expert_back = expert_back.reshape(EXPERTS, windows, CAP, D)
    weights = gate_fixed.astype(jnp.float32).reshape(windows, WINDOW, TOP) / 65536.0
    moe_out = lax.optimization_barrier(jnp.sum(weights[..., None] * expert_out[window_ids, window_index, slot_ids], axis=2)).reshape(TOKENS, D)
    grad_moe = lax.optimization_barrier(jnp.sum(weights[..., None] * expert_back[window_ids, window_index, slot_ids], axis=2)).reshape(TOKENS, D)
    second_out = (y_second.astype(jnp.float32) - moe_out).astype(jnp.bfloat16)
    total_grad = grad_first.astype(jnp.float32) + rms_back(first_in, gain_moe, grad_moe)
    grad_first_out = total_grad.astype(jnp.bfloat16)
    second = second_out.astype(jnp.float32)
    attn_in = (second * rms_scale(second) * gain_attn).astype(jnp.bfloat16)
    queries = jnp.dot(attn_in, w_query, preferred_element_type=jnp.float32).astype(jnp.bfloat16)
    latent = jnp.dot(attn_in, w_latent, preferred_element_type=jnp.float32).astype(jnp.bfloat16)
    latent_f = latent.astype(jnp.float32)
    latent_norm = (latent_f * rms_scale(latent_f) * gain_latent).astype(jnp.bfloat16)
    key_rows = jnp.dot(latent_norm, w_key_up, preferred_element_type=jnp.float32).astype(jnp.bfloat16)
    value_rows = jnp.dot(latent_norm, w_value_up, preferred_element_type=jnp.float32).astype(jnp.bfloat16)
    head_shape = (windows, WINDOW, HEADS, HEAD_DIM)
    query_heads = queries.reshape(head_shape).astype(jnp.float32)
    key_heads = key_rows.reshape(head_shape).astype(jnp.float32)
    value_heads = value_rows.reshape(head_shape).astype(jnp.float32)
    scale_factor = 1.0 / math.sqrt(HEAD_DIM)
    raw_scores = jnp.einsum('nqhk,nshk->nhqs', query_heads, key_heads) * scale_factor
    bounded = jnp.tanh(raw_scores / soft_limit)
    positions = jnp.arange(WINDOW)
    allowed = positions[None, :] <= positions[:, None]
    exp_scores = jnp.where(allowed[None, None], jnp.exp(soft_limit * bounded), 0.0)
    probs_full = exp_scores / lax.optimization_barrier(jnp.sum(exp_scores, axis=-1, keepdims=True))
    probs_low = rounded(probs_full)
    mixed_heads = jnp.einsum('nhqs,nshk->nqhk', probs_low, value_heads).astype(jnp.bfloat16)
    attn_out = jnp.dot(mixed_heads.reshape(TOKENS, HEADS * HEAD_DIM), w_out, preferred_element_type=jnp.float32)
    first_out = (first_in - attn_out).astype(jnp.bfloat16)
    grad_mixed = jnp.dot(grad_first_out, w_out.T, preferred_element_type=jnp.float32).astype(jnp.bfloat16)
    grad_heads = grad_mixed.reshape(head_shape).astype(jnp.float32)
    grad_probs = jnp.einsum('nqhk,nshk->nhqs', grad_heads, value_heads)
    row_delta = lax.optimization_barrier(jnp.sum(probs_full * grad_probs, axis=-1, keepdims=True))
    grad_scores = rounded(probs_full * (grad_probs - row_delta) * (1.0 - bounded * bounded) * scale_factor)
    grad_queries = jnp.einsum('nhqs,nshk->nqhk', grad_scores, key_heads).astype(jnp.bfloat16)
    grad_keys = jnp.einsum('nhqs,nqhk->nshk', grad_scores, query_heads).astype(jnp.bfloat16)
    grad_values = jnp.einsum('nhqs,nqhk->nshk', probs_low, grad_heads).astype(jnp.bfloat16)
    flat_width = HEADS * HEAD_DIM
    grad_latent_norm = jnp.dot(grad_keys.reshape(TOKENS, flat_width), w_key_up.T, preferred_element_type=jnp.float32)
    grad_latent_norm = grad_latent_norm + jnp.dot(grad_values.reshape(TOKENS, flat_width), w_value_up.T, preferred_element_type=jnp.float32)
    grad_latent = rms_back(latent_f, gain_latent, grad_latent_norm).astype(jnp.bfloat16)
    grad_attn_in = jnp.dot(grad_queries.reshape(TOKENS, flat_width), w_query.T, preferred_element_type=jnp.float32)
    grad_attn_in = grad_attn_in + jnp.dot(grad_latent, w_latent.T, preferred_element_type=jnp.float32)
    grad_second_out = (grad_second.astype(jnp.float32) + rms_back(second, gain_attn, grad_attn_in)).astype(jnp.bfloat16)
    return (first_out, second_out, grad_first_out, grad_second_out)
```

```python
import math

import jax
import jax.numpy as jnp
from jax import lax
from jax.sharding import PartitionSpec as P

HEAD_DIM = 128
TOP = 6
AXES = ("exp", "ctx")

epsilon = 1e-06
soft_limit = 5.0


def rms_scale(row_data):
    return lax.rsqrt(jnp.mean(row_data * row_data, axis=-1, keepdims=True) + epsilon)


def rms_back(row_data, gain_vec, grad_in):
    factor = rms_scale(row_data)
    weighted = gain_vec * grad_in
    inner_mean = jnp.mean(weighted * row_data, axis=-1, keepdims=True)
    return factor * weighted - row_data * (factor * factor * factor) * inner_mean


class Net:
    def __init__(self, exp_count, ctx_count):
        self.exp_count, self.ctx_count = exp_count, ctx_count
        self.outer = exp_count // 4
        self.bits = ctx_count.bit_length() - 1
        ctx_masks = [(0, 1 << i) for i in range(self.bits)]
        self.rounds = list(zip([(2, 0)] + ctx_masks, ctx_masks + [(2, 0)]))
        self.odd = (lax.axis_index("exp") & 1) == 1
        self.ctx = lax.axis_index("ctx")

    def swap(self, value, even, odd=None):
        masks = (even, even if odd is None else odd)
        pairs = []
        for e in range(self.exp_count):
            for c in range(self.ctx_count):
                me, mc = masks[e & 1]
                pairs.append((e * self.ctx_count + c, (e ^ me) * self.ctx_count + (c ^ mc)))
        return lax.ppermute(value, AXES, pairs)

    def gather(self, block):
        shape = block.shape
        held = jnp.stack([block] + [self.swap(block, (k << 2, 0)) for k in range(1, self.outer)])
        for even, odd in self.rounds:
            held = jnp.stack([held, self.swap(held, even, odd)])
        a = held.reshape((2, self.ctx_count, self.outer) + shape)
        b = held.reshape((self.ctx_count, 2, self.outer) + shape).swapaxes(0, 1)
        held = jnp.where(self.odd, a, b)
        return jnp.stack([held, self.swap(held, (1, 0))])

    def scatter(self, parts):
        shape = parts.shape[4:]

        def add(mine, sent):
            return mine.astype(jnp.float32) + sent.astype(jnp.float32)

        held = add(parts[0], self.swap(parts[1], (1, 0))).astype(parts.dtype)
        dims = (2,) * (self.bits + 1) + (self.outer,) + shape
        held = jnp.where(self.odd, held.reshape(dims), held.swapaxes(0, 1).reshape(dims))
        for even, odd in reversed(self.rounds):
            held = add(held[0], self.swap(held[1], even, odd)).astype(parts.dtype)
        total = held[0].astype(jnp.float32)
        for k in range(1, self.outer):
            total = total + self.swap(held[k], (k << 2, 0)).astype(jnp.float32)
        return total

    def ctx_gather(self, block):
        held = block[None]
        for i in range(self.bits):
            held = jnp.concatenate([held, self.swap(held, (0, 1 << i))])
        return held

    def ordered(self, held, axis=0):
        shape = held.shape
        held = held.reshape(shape[:axis] + (2,) * self.bits + shape[axis + 1 :])
        for i in range(self.bits):
            at = axis + self.bits - 1 - i
            held = jnp.where((self.ctx >> i) & 1 == 1, jnp.flip(held, at), held)
        return held.reshape(shape)

    def ctx_full(self, block):
        held = self.ordered(self.ctx_gather(block))
        return jnp.concatenate([held[i] for i in range(self.ctx_count)], axis=-1)

    def ctx_sum_own(self, parts):
        held = self.ordered(parts)
        for i in reversed(range(self.bits)):
            half = held.shape[0] // 2
            held = held[:half].astype(jnp.float32) + self.swap(held[half:], (0, 1 << i)).astype(jnp.float32)
            if i:
                held = held.astype(parts.dtype)
        return held[0].astype(jnp.float32)


def mm(a, b):
    return jnp.dot(a, b, preferred_element_type=jnp.float32)


def mm_t(a, b):
    return lax.dot_general(a, b, (((1,), (1,)), ((), ())), preferred_element_type=jnp.float32)


def moe_by_route(net, y_first, grad_second, expert_ids, gate_fixed, gain_moe, w_gate, w_up, w_down, capacity):
    exp_count, local_experts = net.exp_count, w_gate.shape[0]
    expert_count = exp_count * local_experts
    window_len, own_cols = y_first.shape
    width = own_cols * net.ctx_count
    bf = jnp.bfloat16
    full_first, full_gsecond = net.ctx_full(y_first), net.ctx_full(grad_second)
    first_in = full_first.astype(jnp.float32)
    normed = (first_in * rms_scale(first_in) * gain_moe).astype(bf)
    flat_ids = expert_ids.reshape(-1)
    onehot = (flat_ids[:, None] == jnp.arange(expert_count)[None, :]).astype(jnp.int32)
    slots = jnp.sum((jnp.cumsum(onehot, axis=0) - onehot) * onehot, axis=1)
    flat_slots = flat_ids * capacity + slots
    hits = (jnp.arange(expert_count * capacity)[:, None] == flat_slots[None, :]).astype(bf)
    chooser = jnp.max(hits.reshape(expert_count * capacity, window_len, TOP), axis=2)

    def send(rows):
        rows = mm(chooser, rows).astype(bf).reshape(expert_count, capacity, width)
        rows = lax.all_to_all(rows, "exp", split_axis=0, concat_axis=0, tiled=True)
        return rows.reshape(exp_count, local_experts, capacity, width)

    def back(rows):
        rows = rows.astype(bf).reshape(expert_count, capacity, width)
        rows = lax.all_to_all(rows, "exp", split_axis=0, concat_axis=0, tiled=True)
        picked = jnp.take(rows.reshape(expert_count * capacity, width), flat_slots, axis=0)
        picked = picked.reshape(window_len, TOP, width).astype(jnp.float32)
        total = jnp.sum(gate_fixed.astype(jnp.float32)[:, :, None] / 65536.0 * picked, axis=1)
        return net.ctx_sum_own(total.astype(bf).reshape(window_len, net.ctx_count, own_cols).swapaxes(0, 1))

    def dots(spec, a, b):
        return jnp.einsum(spec, a, b, preferred_element_type=jnp.float32)

    rows, grads = send(normed), send(full_gsecond)
    gate_proj, up_proj = dots("secd,edf->secf", rows, w_gate), dots("secd,edf->secf", rows, w_up)
    sig = jax.nn.sigmoid(gate_proj)
    moe_own = back(dots("secf,efd->secd", (gate_proj * sig * up_proj).astype(bf), w_down))
    grad_hidden = dots("secd,efd->secf", grads, w_down)
    grad_gate = (grad_hidden * up_proj * sig * (1.0 + gate_proj * (1.0 - sig))).astype(bf)
    grad_up = (grad_hidden * gate_proj * sig).astype(bf)
    grad_own = back(dots("secf,edf->secd", grad_gate, w_gate) + dots("secf,edf->secd", grad_up, w_up))
    return full_first, moe_own, grad_own


def moe_by_token(net, y_first, grad_second, expert_ids, gate_fixed, gain_moe, w_gate, w_up, w_down, capacity):
    exp_count, ctx_count, local_experts = net.exp_count, net.ctx_count, w_gate.shape[0]
    window_len, own_cols = y_first.shape
    model_width = own_cols * ctx_count
    bf = jnp.bfloat16
    high, low = gate_fixed // 256, gate_fixed % 256
    table = jnp.concatenate([expert_ids, high, low], axis=1).T.astype(bf)
    table_rows = -(-3 * TOP * window_len // own_cols)
    pad_rows = -(-table_rows // 8) * 8
    flat = jnp.pad(table.reshape(-1), (0, pad_rows * own_cols - 3 * TOP * window_len))
    block = jnp.concatenate([y_first, flat.reshape(pad_rows, own_cols)], axis=0)
    got_first = net.gather(block)
    got_gsecond = net.gather(grad_second)
    first_blocks = got_first[..., :window_len, :]
    tables = got_first[:, :, 0, :, window_len:, :].reshape(exp_count, -1)[:, : 3 * TOP * window_len]
    tables = tables.reshape(exp_count, 3, TOP, window_len).astype(jnp.int32)
    route_ids = tables[:, 0]
    route_weights = (tables[:, 1] * 256 + tables[:, 2]).astype(jnp.float32) / 65536.0

    earlier = (jnp.arange(window_len)[:, None] < jnp.arange(window_len)[None, :]).astype(bf)

    def expert(i):
        label = lax.axis_index("exp") * local_experts + i
        named = route_ids == label
        hit = jnp.any(named, axis=1)
        weight = jnp.sum(jnp.where(named, route_weights, 0.0), axis=1)
        slots = mm(hit.astype(bf), earlier).astype(jnp.int32)
        pick = hit[:, None, :] & (slots[:, None, :] == jnp.arange(capacity)[None, :, None])
        row_weight = jnp.sum(jnp.where(pick, weight[:, None, :], 0.0), axis=2).reshape(-1, 1)
        pick = pick.astype(bf)

        def rows_of(blocks):
            b = blocks.swapaxes(2, 3).reshape(exp_count, ctx_count, window_len, own_cols)
            rows = jnp.einsum("wst,whtd->whsd", pick, b, preferred_element_type=jnp.float32)
            rows = net.ordered(rows.astype(bf), 1)
            return rows.swapaxes(1, 2).reshape(exp_count * capacity, model_width)

        def dense_of(rows):
            r = rows.astype(bf).reshape(exp_count, capacity, ctx_count, own_cols).swapaxes(1, 2)
            r = net.ordered(r, 1)
            d = jnp.einsum("wst,whsd->whtd", pick, r, preferred_element_type=jnp.float32)
            d = d.reshape(2, 2, exp_count // 4, ctx_count, window_len, own_cols).swapaxes(2, 3)
            return d.astype(bf)

        rows = rows_of(first_blocks).astype(jnp.float32)
        rows = (rows * rms_scale(rows) * gain_moe).astype(bf)
        gate_proj, up_proj = mm(rows, w_gate[i]), mm(rows, w_up[i])
        sig = jax.nn.sigmoid(gate_proj)
        hidden = (row_weight * gate_proj * sig * up_proj).astype(bf)
        part_out = dense_of(mm(hidden, w_down[i]))
        grads = rows_of(got_gsecond)
        grad_hidden = mm_t(grads, w_down[i]) * row_weight
        grad_gate = (grad_hidden * up_proj * sig * (1.0 + gate_proj * (1.0 - sig))).astype(bf)
        grad_up = (grad_hidden * gate_proj * sig).astype(bf)
        part_back = dense_of(mm_t(grad_gate, w_gate[i]) + mm_t(grad_up, w_up[i]))
        return part_out, part_back

    outs = [expert(i) for i in range(local_experts)]
    part_out = sum([o[0] for o in outs[1:]], outs[0][0])
    part_back = sum([o[1] for o in outs[1:]], outs[0][1])
    moe_own = net.scatter(part_out)
    grad_moe_own = net.scatter(part_back)
    blocks = net.ordered(first_blocks[0, 0, :, 0])
    full_first = jnp.concatenate([blocks[i] for i in range(ctx_count)], -1)
    return full_first, moe_own, grad_moe_own


def local(
    y_first,
    y_second,
    grad_first,
    grad_second,
    expert_ids,
    gate_fixed,
    gain_attn,
    gain_latent,
    gain_moe,
    w_query,
    w_latent,
    w_key_up,
    w_value_up,
    w_out,
    w_gate,
    w_up,
    w_down,
):
    ctx_count = lax.axis_size("ctx")
    exp_count = lax.axis_size("exp")
    ctx_index = lax.axis_index("ctx")
    net = Net(exp_count, ctx_count)
    local_experts = w_gate.shape[0]
    expert_count = exp_count * local_experts
    window_len, own_cols = y_first.shape
    model_width = own_cols * ctx_count
    capacity = ctx_count * (
        (window_len * TOP * 4 + 3 * expert_count * ctx_count - 1) // (3 * expert_count * ctx_count)
    )
    bf = jnp.bfloat16
    few = exp_count * local_experts <= 4 * TOP and exp_count % 4 == 0
    moe = moe_by_token if few else moe_by_route
    full_first, moe_own, grad_moe_own = moe(
        net, y_first, grad_second, expert_ids, gate_fixed, gain_moe, w_gate, w_up, w_down, capacity
    )
    w_latent_full = net.ctx_full(w_latent)
    first_in = full_first.astype(jnp.float32)
    full_gfirst = net.ctx_full(grad_first)
    second_out = (y_second.astype(jnp.float32) - moe_own).astype(bf)
    second = net.ctx_full(second_out).astype(jnp.float32)
    grad_moe = net.ctx_full(grad_moe_own.astype(bf)).astype(jnp.float32)
    total_grad = full_gfirst.astype(jnp.float32) + rms_back(first_in, gain_moe, grad_moe)
    grad_first_full = total_grad.astype(bf)
    attn_in = (second * rms_scale(second) * gain_attn).astype(bf)
    queries = mm(attn_in, w_query).astype(bf)
    latent = mm(attn_in, w_latent_full).astype(bf)
    latent_f = latent.astype(jnp.float32)
    latent_norm = (latent_f * rms_scale(latent_f) * gain_latent).astype(bf)
    key_rows = mm(latent_norm, w_key_up).astype(bf)
    value_rows = mm(latent_norm, w_value_up).astype(bf)
    local_heads = w_query.shape[1] // HEAD_DIM
    scale_factor = 1.0 / math.sqrt(HEAD_DIM)
    positions = jnp.arange(window_len)
    allowed = positions[None, :] <= positions[:, None]
    grad_mixed = mm_t(grad_first_full, w_out).astype(bf)
    head_shape = (window_len, local_heads, HEAD_DIM)
    q_h, k_h, v_h = [t.reshape(head_shape) for t in (queries, key_rows, value_rows)]
    g_h = grad_mixed.reshape(head_shape)
    raw = jnp.einsum("qhk,shk->hqs", q_h, k_h, preferred_element_type=jnp.float32) * scale_factor
    bounded = jnp.tanh(raw / soft_limit)
    exp_scores = jnp.where(allowed[None], jnp.exp(soft_limit * bounded), 0.0)
    probs = exp_scores / jnp.sum(exp_scores, axis=-1, keepdims=True)
    probs_low = probs.astype(bf)
    mixed = jnp.einsum("hqs,shk->qhk", probs_low, v_h, preferred_element_type=jnp.float32)
    mixed = mixed.astype(bf).reshape(window_len, -1)
    attn_part = mm(mixed, w_out).astype(bf).reshape(window_len, ctx_count, own_cols).swapaxes(0, 1)
    attn_own = net.ctx_sum_own(attn_part)
    first_out = (y_first.astype(jnp.float32) - attn_own).astype(bf)
    g_p = jnp.einsum("qhk,shk->hqs", g_h, v_h, preferred_element_type=jnp.float32)
    delta = jnp.sum(probs * g_p, axis=-1, keepdims=True)
    g_s = (probs * (g_p - delta) * (1.0 - bounded * bounded) * scale_factor).astype(bf)
    g_q = jnp.einsum("hqs,shk->qhk", g_s, k_h, preferred_element_type=jnp.float32)
    g_k = jnp.einsum("hqs,qhk->shk", g_s, q_h, preferred_element_type=jnp.float32)
    g_v = jnp.einsum("hqs,qhk->shk", probs_low, g_h, preferred_element_type=jnp.float32)
    g_q, g_k, g_v = [t.astype(bf).reshape(window_len, -1) for t in (g_q, g_k, g_v)]
    latent_grad = mm_t(g_k, w_key_up) + mm_t(g_v, w_value_up)
    grad_latent = rms_back(latent_f, gain_latent, latent_grad).astype(bf)
    input_grad = mm_t(g_q, w_query) + mm_t(grad_latent, w_latent_full)
    back = rms_back(second, gain_attn, input_grad).astype(bf)
    back = back.reshape(window_len, ctx_count, own_cols).swapaxes(0, 1)
    own_back = net.ctx_sum_own(back)
    grad_second_out = (grad_second.astype(jnp.float32) + own_back).astype(bf)
    grad_first_out = lax.dynamic_slice_in_dim(grad_first_full, ctx_index * own_cols, own_cols, 1)
    return (first_out, second_out, grad_first_out, grad_second_out)


def solution(mesh):
    placed = (
        P("exp", "ctx"),
        P("exp", "ctx"),
        P("exp", "ctx"),
        P("exp", "ctx"),
        P("exp", None),
        P("exp", None),
        P(),
        P(),
        P(),
        P(None, "ctx"),
        P(None, "ctx"),
        P(None, "ctx"),
        P(None, "ctx"),
        P("ctx", None),
        P("exp", None, "ctx"),
        P("exp", None, "ctx"),
        P("exp", "ctx", None),
    )
    return jax.shard_map(
        local,
        mesh=mesh,
        in_specs=placed,
        out_specs=(P("exp", "ctx"), P("exp", "ctx"), P("exp", "ctx"), P("exp", "ctx")),
        check_vma=False,
    )
```
